32 devices in a mesh: doc: 4 (over z), feat: 8 (over y, x, core).
Axes of the slice: x: 2, y: 2, z: 4, core: 2. Of those that a mesh axis runs over, the one named last changes fastest.
Arguments:
- documents: bfloat16 [512, 512], P('doc', 'feat'), may hold values from -6 to 6
- directions: bfloat16 [512, 32768], P('doc', 'feat'), may hold values from -0.5 to 0.5
- phase: float32 [32768], P('feat'), may hold values from -3.140625 to 3.140625
- amplitude: float32 [32768], P('feat'), may hold values from 0.4 to 2.3
- doc_weight: float32 [512], P('doc'), may hold values from 0.5 to 4.2
- labels: int32 [512], P('doc'), may hold values from 0 to 127
Outputs:
- margins: float32 [512, 128], P('doc')
- scaled_weights: float32 [32768, 128], P('feat')
The draws below stay inside these ranges and needn't reach their ends.
All inputs are finite; a program needn't handle non-finite values.
Results may differ from the reference program's by a relative error of at most 0.0003.
Values may be sent and summed in bfloat16 or wider, within the bound.
A program may use at most 64 MiB of HBM per device.

```python
import jax
import jax.numpy as jnp
from jax import lax

F = 512
W = 32768
C = 128
DOC_DEV = 128
ITERS = 3
NEWTON = 3
NDOC = 512
N_DOC = 4
N_FEAT = 8


def draw_amplitude(key, part):
    ramp = 0.6 + 1.2 * jnp.arange(W, dtype=jnp.float32) / (W - 1)
    spread = jax.random.uniform(key, (W,), jnp.float32, 0.8, 1.2)
    return ramp * spread


def draw_doc_weight(key, part):
    ramp = 1.0 + 2.0 * jnp.arange(NDOC, dtype=jnp.float32) / (NDOC - 1)
    spread = jax.random.uniform(key, (NDOC,), jnp.float32, 0.7, 1.3)
    return ramp * spread


def with_ends(entries, own_key, smallest, high):
    longest = entries.shape.index(max(entries.shape))
    spots = []
    for shift in (0, 1):
        where = [jax.random.randint(jax.random.fold_in(own_key, axis), (), 0, length) for axis, length in enumerate(entries.shape)]
        where[longest] = (where[longest] + shift) % entries.shape[longest]
        spots.append(tuple(where))
    return entries.at[spots[0]].set(smallest).at[spots[1]].set(high)


def block_scale(key, extent, shards, smallest, largest):
    def one(position, parts):
        heights = jax.random.uniform(jax.random.fold_in(jax.random.fold_in(key, 6), position), (parts,), jnp.float32, smallest / len(shards), largest / len(shards))
        return jnp.repeat(jnp.exp(heights), extent[position] // parts).reshape((-1,) + (1,) * (len(extent) - position - 1))

    level = one(*shards[0])
    for cut in shards[1:]:
        level = level * one(*cut)
    return level


def normal_values(stream_key, shape, width, most, shards=(), held_as=jnp.bfloat16):
    values = width * jax.random.normal(stream_key, shape, jnp.float32)
    if shards:
        values = values * block_scale(stream_key, shape, shards, -0.22, 0.18)
    return jnp.clip(values, -most, most).astype(held_as)


def setup_inputs(seed: int = 0) -> dict:
    keys = jax.random.split(jax.random.key(seed), 7)
    documents = normal_values(keys[0], (NDOC, F), 1.0, 6.0, ((0, 4), (1, 8)))
    directions = normal_values(keys[1], (F, W), (F // 4) ** -0.5, 0.5, ((0, 4), (1, 8)))
    phase = jnp.clip(jax.random.uniform(keys[2], (W,), jnp.float32, -3.140625, 3.140625), -3.140625, 3.140625)
    amplitude = draw_amplitude(jax.random.fold_in(keys[6], 71), 0)
    doc_weight = draw_doc_weight(jax.random.fold_in(keys[6], 71), 0)
    labels = with_ends(jax.random.randint(keys[5], (NDOC,), 0, C), jax.random.fold_in(keys[5], 1), 0, C - 1).astype(jnp.int32)
    return dict(documents=documents, directions=directions, phase=phase, amplitude=amplitude, doc_weight=doc_weight, labels=labels)


shrink_level = 0.1
ratio_floor = 1e-06

def feature_tile(documents, directions, phase, amplitude, row_block, col_block):
    width_tile = W // N_FEAT
    doc_rows = lax.dynamic_slice_in_dim(documents, (row_block * DOC_DEV).astype(jnp.int32), DOC_DEV, 0)
    dir_cols = lax.dynamic_slice_in_dim(directions, (col_block * width_tile).astype(jnp.int32), width_tile, 1)
    phase_cols = lax.dynamic_slice_in_dim(phase, (col_block * width_tile).astype(jnp.int32), width_tile, 0)
    amp_cols = lax.dynamic_slice_in_dim(amplitude, (col_block * width_tile).astype(jnp.int32), width_tile, 0)
    angles = jnp.dot(doc_rows.astype(jnp.float32), dir_cols.astype(jnp.float32), preferred_element_type=jnp.float32)
    return jnp.sqrt(2.0 / width_tile) * amp_cols * jnp.cos(angles + phase_cols)

def project_tile(features, factor, start, target):
    residue = target - jnp.dot(features, start, precision=lax.Precision.HIGHEST)
    halfway = lax.linalg.triangular_solve(factor, residue, left_side=True, lower=True)
    solved = lax.linalg.triangular_solve(factor, halfway, left_side=True, lower=True, transpose_a=True)
    new_copy = start + lax.dot_general(features, solved, (((0,), (0,)), ((), ())), precision=lax.Precision.HIGHEST)
    new_part = jnp.dot(features, new_copy, precision=lax.Precision.HIGHEST)
    return (new_copy, new_part)

def logistic_prox(target, signs, weight_ratio):
    current = target
    for newton_step in range(NEWTON):
        chance = jax.nn.sigmoid(-signs * current)
        gradient = current - target - weight_ratio * signs * chance
        current = current - gradient / (1.0 + weight_ratio * chance * (1.0 - chance))
    return current

def shrink_values(target, limit):
    return target - jnp.clip(target, -limit, limit)

def reference(documents, directions, phase, amplitude, doc_weight, labels):
    width_tile = W // N_FEAT
    tile_count = N_DOC * N_FEAT
    tile_index = jnp.arange(tile_count, dtype=jnp.int32)

    def factor_tile(tile):
        features = feature_tile(documents, directions, phase, amplitude, tile // N_FEAT, tile % N_FEAT)
        gram = jnp.eye(DOC_DEV, dtype=jnp.float32) + lax.dot_general(features, features, (((1,), (1,)), ((), ())), precision=lax.Precision.HIGHEST)
        return jnp.linalg.cholesky(gram)
    factors = lax.map(factor_tile, tile_index)
    signs = jnp.where(labels[:, None] == jnp.arange(C, dtype=jnp.int32)[None, :], 1.0, -1.0).astype(jnp.float32)
    loss_weight = doc_weight[:, None]
    rho = jnp.float32(1.0)
    margins = logistic_prox(jnp.zeros((NDOC, C), jnp.float32), signs, loss_weight / rho)
    sums = jnp.zeros((NDOC, C), jnp.float32)
    duals_y = jnp.zeros((NDOC, C), jnp.float32)
    duals_x = jnp.zeros((N_DOC, N_FEAT, width_tile, C), jnp.float32)
    partial_value = jnp.zeros((N_DOC, N_FEAT, DOC_DEV, C), jnp.float32)
    weights = jnp.zeros((N_FEAT, width_tile, C), jnp.float32)
    for step in range(ITERS):
        fix_blocks = ((margins - duals_y - sums) / N_FEAT).reshape(N_DOC, DOC_DEV, C)

        def tile_step(tile):
            row_block = tile // N_FEAT
            col_block = tile % N_FEAT
            features = feature_tile(documents, directions, phase, amplitude, row_block, col_block)
            start = weights[col_block] - duals_x[row_block, col_block]
            target = partial_value[row_block, col_block] + fix_blocks[row_block]
            return project_tile(features, factors[tile], start, target)
        new_copy, new_part = lax.map(tile_step, tile_index)
        new_copy = new_copy.reshape(N_DOC, N_FEAT, width_tile, C)
        partial_value = new_part.reshape(N_DOC, N_FEAT, DOC_DEV, C)
        sums = lax.optimization_barrier(jnp.sum(partial_value, axis=1)).reshape(NDOC, C)
        old_weights = weights
        old_margins = margins
        weights = shrink_values(lax.optimization_barrier(jnp.sum(new_copy + duals_x, axis=0)) / N_DOC, shrink_level / (rho * N_DOC))
        margins = logistic_prox(sums + duals_y, signs, loss_weight / rho)
        duals_x = duals_x + new_copy - weights[None]
        duals_y = duals_y + sums - margins
        if step + 1 < ITERS:
            primal = jnp.sum((new_copy - weights[None]) ** 2) + jnp.sum((sums - margins) ** 2)
            dual_norm = rho * rho * (N_DOC * jnp.sum((weights - old_weights) ** 2) + jnp.sum((margins - old_margins) ** 2))
            growth = ((primal + ratio_floor) / (dual_norm + ratio_floor)) ** 0.25
            rho = rho * growth
            duals_x = duals_x / growth
            duals_y = duals_y / growth
    return (margins, N_FEAT * weights.reshape(W, C))
```

```python
import jax
import jax.numpy as jnp
from jax import lax
from jax.sharding import PartitionSpec as P

C = 128
ITERS = 3
NEWTON = 3
HI = lax.Precision.HIGHEST

shrink_level = 0.1
ratio_floor = 1e-06


def logistic_prox(target, signs, weight_ratio):
    current = target
    for newton_step in range(NEWTON):
        chance = jax.nn.sigmoid(-signs * current)
        gradient = current - target - weight_ratio * signs * chance
        current = current - gradient / (1.0 + weight_ratio * chance * (1.0 - chance))
    return current


def shrink_values(target, limit):
    return target - jnp.clip(target, -limit, limit)


def per_device(documents, directions, phase, amplitude, doc_weight, labels):
    doc_count = documents.shape[0]
    width_tile = directions.shape[1]
    num_feat = lax.axis_size("feat")
    num_doc = lax.axis_size("doc")
    chunk = width_tile // num_doc
    row = lax.axis_index("doc")
    doc_rows = lax.all_gather(documents, "feat", axis=1, tiled=True)
    doc_full = lax.all_gather(doc_rows, "doc", axis=0, tiled=True)
    dir_chunk = lax.all_to_all(directions, "doc", split_axis=1, concat_axis=0, tiled=True)
    phase_c = lax.dynamic_slice_in_dim(phase, row * chunk, chunk, 0)
    amp_c = lax.dynamic_slice_in_dim(amplitude, row * chunk, chunk, 0)
    angles = jnp.dot(doc_full, dir_chunk, preferred_element_type=jnp.float32)
    features = jnp.sqrt(2.0 / width_tile) * amp_c * jnp.cos(angles + phase_c)
    blocks = features.reshape(num_doc, doc_count, chunk)
    gram = jnp.einsum("iac,ibc->iab", blocks, blocks, precision=HI)
    gram = lax.psum_scatter(gram, "doc", scatter_dimension=0, tiled=True)[0]
    eye = jnp.eye(doc_count, dtype=jnp.float32)
    factor = jnp.linalg.cholesky(eye + gram)
    lower_inv = lax.linalg.triangular_solve(factor, eye, left_side=True, lower=True)
    inverse = lax.dot_general(lower_inv, lower_inv, (((0,), (0,)), ((), ())), precision=HI)
    signs = jnp.where(labels[:, None] == jnp.arange(C, dtype=jnp.int32)[None, :], 1.0, -1.0).astype(
        jnp.float32
    )
    share_rows = doc_count // num_feat
    offset = lax.axis_index("feat") * share_rows
    signs = lax.dynamic_slice_in_dim(signs, offset, share_rows, 0)
    weight = lax.dynamic_slice_in_dim(doc_weight, offset, share_rows, 0)[:, None]
    rho = jnp.float32(1.0)
    margins = logistic_prox(jnp.zeros(signs.shape, jnp.float32), signs, weight / rho)
    sums = jnp.zeros(signs.shape, jnp.float32)
    duals_y = jnp.zeros(signs.shape, jnp.float32)
    part = jnp.zeros((doc_count, C), jnp.float32)
    image = jnp.zeros((doc_count, C), jnp.float32)
    weights = jnp.zeros((chunk, C), jnp.float32)
    product = jnp.zeros((doc_count, C), jnp.float32)
    for step in range(ITERS):
        correction = (margins - duals_y - sums) / num_feat
        correction = lax.all_gather(correction, "feat", axis=0, tiled=True)
        target = part + correction
        residue = target - image
        solved = jnp.dot(inverse, residue, precision=HI)
        applied = residue - solved
        part = target - solved
        sums = lax.psum_scatter(part, "feat", scatter_dimension=0, tiled=True)
        all_solved = lax.all_gather(solved, "doc", axis=0, tiled=True)
        lifted = lax.dot_general(features, all_solved, (((0,), (0,)), ((), ())), precision=HI)
        old_weights = weights
        old_margins = margins
        weights = shrink_values(weights + lifted / num_doc, shrink_level / (rho * num_doc))
        margins = logistic_prox(sums + duals_y, signs, weight / rho)
        duals_y = duals_y + sums - margins
        if step + 1 < ITERS:
            move = old_weights - weights
            if step == 0:
                d_move, d_solved, d_applied, d_lifted = move, solved, applied, lifted
            else:
                d_move = move - last_move / growth
                d_solved = solved - last_solved / growth
                d_applied = applied - last_applied / growth
                d_lifted = lifted - last_lifted / growth
            primal = (
                jnp.sum(num_doc * d_move * d_move + 2.0 * d_move * d_lifted)
                + jnp.sum(d_solved * d_applied)
                + jnp.sum((sums - margins) ** 2)
            )
            dual = num_doc * jnp.sum(move**2) + jnp.sum((margins - old_margins) ** 2)
            primal, dual = lax.psum((primal, dual), ("doc", "feat"))
            primal = jnp.maximum(primal, 0.0)
            new_product = jnp.dot(features, weights, precision=HI)
            new_product = lax.psum_scatter(new_product, "doc", scatter_dimension=0, tiled=True)
            growth = ((primal + ratio_floor) / (rho * rho * dual + ratio_floor)) ** 0.25
            rho = rho * growth
            duals_y = duals_y / growth
            image = new_product - (product - new_product + applied) / growth
            product = new_product
            last_move, last_solved, last_applied, last_lifted = move, solved, applied, lifted
    margins = lax.all_gather(margins, "feat", axis=0, tiled=True)
    weights = lax.all_gather(num_feat * weights, "doc", axis=0, tiled=True)
    return (margins, weights)


def solution(mesh):
    in_specs = (P("doc", "feat"), P("doc", "feat"), P("feat"), P("feat"), P("doc"), P("doc"))
    out_specs = (P("doc", None), P("feat", None))
    return jax.shard_map(
        per_device, mesh=mesh, in_specs=in_specs, out_specs=out_specs, check_vma=False
    )
```

```python
import functools

import jax
import jax.numpy as jnp
from jax import lax
from jax.experimental import pallas as pl
from jax.experimental.pallas import tpu as pltpu
from jax.sharding import PartitionSpec as P

C = 128
ITERS = 3
NEWTON = 3
HI = lax.Precision.HIGHEST
MESH = pl.DeviceIdType.MESH

shrink_level = 0.1
ratio_floor = 1e-06


def logistic_prox(target, signs, weight_ratio):
    current = target
    for newton_step in range(NEWTON):
        chance = 1.0 / (1.0 + jnp.exp(signs * current))
        gradient = current - target - weight_ratio * signs * chance
        current = current - gradient / (1.0 + weight_ratio * chance * (1.0 - chance))
    return current


def shrink_values(target, limit):
    return target - jnp.minimum(jnp.maximum(target, -limit), limit)


def cosine(angle):
    turns = jnp.floor(angle * 0.3183098861837907 + 0.5)
    rest = angle - turns * 3.140625
    rest = rest - turns * 9.67502593994140625e-4
    rest = rest - turns * 1.509957990978376432e-7
    odd = turns - 2.0 * jnp.floor(turns * 0.5)
    sq = rest * rest
    poly = 2.08767569878681e-9
    poly = poly * sq - 2.755731922398589e-7
    poly = poly * sq + 2.48015873015873e-5
    poly = poly * sq - 1.388888888888889e-3
    poly = poly * sq + 4.1666666666666664e-2
    poly = poly * sq - 0.5
    poly = poly * sq + 1.0
    return poly * (1.0 - 2.0 * odd)


def remote(src, dst, send_sem, recv_sem, axis, peer):
    return pltpu.make_async_remote_copy(
        src_ref=src,
        dst_ref=dst,
        send_sem=send_sem,
        recv_sem=recv_sem,
        device_id={axis: peer},
        device_id_type=MESH,
    )


def greet(num_doc, num_feat):
    barrier = pltpu.get_barrier_semaphore()
    for axis, size in (("doc", num_doc), ("feat", num_feat)):
        me = lax.axis_index(axis)
        for k in range(1, size):
            pl.semaphore_signal(
                barrier, inc=1, device_id={axis: lax.rem(me + k, size)}, device_id_type=MESH
            )
    pl.semaphore_wait(barrier, num_doc + num_feat - 2)


class Channel:
    def __init__(self, sems, axis, size):
        self.sems, self.axis, self.size = sems, axis, size
        self.me = lax.axis_index(axis)
        self.pending = []

    def peers(self):
        return [lax.rem(self.me + k, self.size) for k in range(1, self.size)]

    def send(self, slot, peer, src, dst):
        copy = remote(
            src, dst, self.sems.at[0, slot, peer], self.sems.at[1, slot, self.me], self.axis, peer
        )
        copy.start()
        self.pending.append(copy)

    def arrived(self, slot, peer, ref):
        remote(
            ref, ref, self.sems.at[0, slot, peer], self.sems.at[1, slot, peer], self.axis, peer
        ).wait_recv()

    def drain(self):
        for copy in self.pending:
            copy.wait_send()


def build_kernel(
    num_doc, num_feat, subs, scale,
    docs_ref, dir_ref, phase_ref, amp_ref,
    feat_ref, featt_ref, gram_ref,
    dpart, drow, dirs, gsend, grecv, part_sems, row_sems, dir_sems, gram_sems, local_sem,
):
    n = docs_ref.shape[0]
    chunk = dirs.shape[2]
    wide = chunk // subs
    me = lax.axis_index("doc")
    fme = lax.axis_index("feat")
    greet(num_doc, num_feat)
    ch_part = Channel(part_sems, "feat", num_feat)
    ch_row = Channel(row_sems, "doc", num_doc)
    ch_dir = Channel(dir_sems, "doc", num_doc)
    ch_gram = Channel(gram_sems, "doc", num_doc)
    for peer in ch_part.peers():
        ch_part.send(0, peer, docs_ref, dpart.at[fme])
    local = pltpu.make_async_copy(
        dir_ref.at[:, pl.ds(pl.multiple_of(me * chunk, chunk), chunk)], dirs.at[me], local_sem
    )
    local.start()
    for s in range(subs):
        for peer in ch_dir.peers():
            cols = pl.ds(pl.multiple_of(peer * chunk + s * wide, wide), wide)
            ch_dir.send(
                s, peer, dir_ref.at[:, cols], dirs.at[me, :, pl.ds(s * wide, wide)]
            )
    dpart[fme] = docs_ref[...]
    for peer in ch_part.peers():
        ch_part.arrived(0, peer, dpart.at[peer])
    row = jnp.concatenate(
        [dpart[k].astype(jnp.float32) for k in range(num_feat)], axis=1
    ).astype(jnp.bfloat16)
    drow[me] = row
    for peer in ch_row.peers():
        ch_row.send(0, peer, drow.at[me], drow.at[me])
    for peer in ch_row.peers():
        ch_row.arrived(0, peer, drow.at[peer])
    local.wait()
    full = drow[...].reshape(num_doc * n, drow.shape[2])
    phase = phase_ref[me]
    amp = scale * amp_ref[me]
    for s in range(subs):
        cols = slice(s * wide, (s + 1) * wide)
        for peer in ch_dir.peers():
            ch_dir.arrived(s, peer, dirs.at[peer, :, pl.ds(s * wide, wide)])
        piece = dirs[:, :, cols].reshape(full.shape[1], wide)
        angles = jnp.dot(full, piece, preferred_element_type=jnp.float32)
        feats = amp[:, cols] * cosine(angles + phase[:, cols])
        feat_ref[:, cols] = feats
        featt_ref[cols, :] = feats.T
        for i in range(num_doc):
            block = feats[i * n : (i + 1) * n]
            term = lax.dot_general(block, block, (((1,), (1,)), ((), ())), precision=HI)
            if s == 0:
                gsend[i] = term
            else:
                gsend[i] += term
    for peer in ch_gram.peers():
        ch_gram.send(0, peer, gsend.at[peer], grecv.at[me])
    grecv[me] = gsend[me]
    for peer in ch_gram.peers():
        ch_gram.arrived(0, peer, grecv.at[peer])
    total = grecv[0]
    for i in range(1, num_doc):
        total += grecv[i]
    rows = lax.broadcasted_iota(jnp.int32, (n, n), 0)
    cols = lax.broadcasted_iota(jnp.int32, (n, n), 1)
    gram_ref[...] = total + jnp.where(rows == cols, 1.0, 0.0)
    for channel in (ch_part, ch_row, ch_dir, ch_gram):
        channel.drain()


def fold(values):
    return jnp.sum(values.reshape(values.shape[0] // 8, 8, values.shape[1]), axis=0)


def total(values):
    return jnp.sum(jnp.sum(values, axis=0, keepdims=True), axis=1, keepdims=True)


def admm_kernel(
    num_doc, num_feat, subs,
    feat_ref, featt_ref, inv_ref, lab_ref, dw_ref,
    m_ref, w_ref,
    solved, part, yrecv, cbuf, psend, precv, sc1, sc2, z, lastmove, lastlift,
    s_sems, y_sems, c_sems, p_sems, sc1_sems, sc2_sems, w_sems,
):
    n = inv_ref.shape[0]
    chunk = z.shape[0]
    share = n // num_feat
    wide = chunk // subs
    me = lax.axis_index("doc")
    fme = lax.axis_index("feat")
    greet(num_doc, num_feat)
    ch_s = Channel(s_sems, "doc", num_doc)
    ch_y = Channel(y_sems, "feat", num_feat)
    ch_c = Channel(c_sems, "feat", num_feat)
    ch_p = Channel(p_sems, "doc", num_doc)
    ch_1 = Channel(sc1_sems, "doc", num_doc)
    ch_2 = Channel(sc2_sems, "feat", num_feat)
    classes = lax.broadcasted_iota(jnp.int32, (n, C), 1)
    all_signs = jnp.where(lab_ref[...] == classes, 1.0, -1.0)
    start = logistic_prox(jnp.zeros((n, C), jnp.float32), all_signs, dw_ref[...])
    own = pl.ds(pl.multiple_of(fme * share, share), share)
    signs = jnp.where(
        lab_ref[own, :] == lax.broadcasted_iota(jnp.int32, (share, C), 1), 1.0, -1.0
    )
    weight = dw_ref[own, :]
    margins = logistic_prox(jnp.zeros((share, C), jnp.float32), signs, weight)
    duals = jnp.zeros((share, C), jnp.float32)
    rho = jnp.ones((1, 1), jnp.float32)
    inv = inv_ref[...]
    target = start / num_feat
    residue = target
    growth = None

    def my_rows(src, s):
        return pl.ds(pl.multiple_of(src * chunk + s * wide, wide), wide)

    def w_copy(direction, src, s, peer):
        ref = w_ref.at[my_rows(src, s), :]
        return remote(
            ref, ref, w_sems.at[direction, 0, src, s], w_sems.at[direction, 1, src, s], "doc", peer
        )

    for step in range(ITERS):
        last = step + 1 == ITERS
        answer = jnp.dot(inv, residue, precision=HI)
        applied = residue - answer
        new_part = target - answer
        solved[step, me] = answer
        part[step] = new_part
        for peer in ch_s.peers():
            ch_s.send(step, peer, solved.at[step, me], solved.at[step, me])
        for peer in ch_y.peers():
            rows = pl.ds(pl.multiple_of(peer * share, share), share)
            ch_y.send(step, peer, part.at[step, rows, :], yrecv.at[step, fme])
        yrecv[step, fme] = part[step, own, :]
        for peer in ch_y.peers():
            ch_y.arrived(step, peer, yrecv.at[step, peer])
        sums = yrecv[step, 0]
        for k in range(1, num_feat):
            sums += yrecv[step, k]
        old_margins = margins
        margins = logistic_prox(sums + duals, signs, weight / rho)
        duals = duals + sums - margins
        cbuf[step, fme, 0] = margins if last else (margins - sums) / num_feat
        cbuf[step, fme, 1] = duals / num_feat
        for peer in ch_c.peers():
            ch_c.send(step, peer, cbuf.at[step, fme], cbuf.at[step, fme])
        for peer in ch_s.peers():
            ch_s.arrived(step, peer, solved.at[step, peer])
        everything = solved[step].reshape(num_doc * n, C)
        limit = shrink_level / (rho * num_doc)
        if not last:
            gap = fold((sums - margins) ** 2) if share > 8 else (sums - margins) ** 2
            shift = (
                fold((margins - old_margins) ** 2) if share > 8 else (margins - old_margins) ** 2
            )
            if step == 0:
                d_answer, d_applied = answer, applied
            else:
                d_answer = answer - last_answer / growth
                d_applied = applied - last_applied / growth
            primal = gap + fold(d_answer * d_applied)
            dual = shift
        for s in range(subs):
            rows = slice(s * wide, (s + 1) * wide)
            lift = jnp.dot(featt_ref[rows, :], everything, precision=HI)
            if step == 0:
                fresh = shrink_values(lift / num_doc, limit)
                move = -fresh
                d_move, d_lift = move, lift
            else:
                old = z[rows, :]
                fresh = shrink_values(old + lift / num_doc, limit)
                if not last:
                    move = old - fresh
                    d_move = move - lastmove[rows, :] / growth
                    d_lift = lift - lastlift[rows, :] / growth
            if last:
                w_ref[my_rows(me, s), :] = num_feat * fresh

                @pl.when(me + 1 < num_doc)
                def _(s=s):
                    w_copy(0, me, s, me + 1).start()

                @pl.when(me >= 1)
                def _(s=s):
                    w_copy(1, me, s, me - 1).start()
            else:
                z[rows, :] = fresh
                lastmove[rows, :] = move
                lastlift[rows, :] = lift
                primal += fold(num_doc * d_move * d_move + 2.0 * d_move * d_lift)
                dual += num_doc * fold(move * move)
        if last:
            break
        sc1[step, me, 0] = primal
        sc1[step, me, 1] = dual
        for peer in ch_1.peers():
            ch_1.send(step, peer, sc1.at[step, me], sc1.at[step, me])
        weights = z[...]
        for i in range(num_doc):
            psend[step, i] = jnp.dot(feat_ref[i * n : (i + 1) * n, :], weights, precision=HI)
        for peer in ch_p.peers():
            ch_p.send(step, peer, psend.at[step, peer], precv.at[step, me])
        precv[step, me] = psend[step, me]
        for peer in ch_1.peers():
            ch_1.arrived(step, peer, sc1.at[step, peer])
        both = sc1[step, 0]
        for i in range(1, num_doc):
            both += sc1[step, i]
        sc2[step, fme] = both
        for peer in ch_2.peers():
            ch_2.send(step, peer, sc2.at[step, fme], sc2.at[step, fme])
        for peer in ch_2.peers():
            ch_2.arrived(step, peer, sc2.at[step, peer])
        both = sc2[step, 0]
        for k in range(1, num_feat):
            both += sc2[step, k]
        primal = jnp.maximum(total(both[0]), 0.0)
        dual = total(both[1])
        last_answer, last_applied = answer, applied
        for peer in ch_c.peers():
            ch_c.arrived(step, peer, cbuf.at[step, peer])
        growth = jnp.sqrt(
            jnp.sqrt((primal + ratio_floor) / (rho * rho * dual + ratio_floor))
        )
        rho = rho * growth
        duals = duals / growth
        fixed = cbuf[step, :, 0].reshape(n, C) - cbuf[step, :, 1].reshape(n, C) / growth
        target = new_part + fixed
        for peer in ch_p.peers():
            ch_p.arrived(step, peer, precv.at[step, peer])
        product = precv[step, 0]
        for i in range(1, num_doc):
            product += precv[step, i]
        previous = jnp.zeros((n, C), jnp.float32) if step == 0 else old_product
        residue = target - (product - (previous - product + applied) / growth)
        old_product = product
    for hop in range(1, num_doc):
        for s in range(subs):

            @pl.when(me >= hop)
            def _(hop=hop, s=s):
                w_copy(0, me - hop, s, me).wait_recv()

                @pl.when(me + 1 < num_doc)
                def _():
                    w_copy(0, me - hop, s, me + 1).start()

            @pl.when(me + hop < num_doc)
            def _(hop=hop, s=s):
                w_copy(1, me + hop, s, me).wait_recv()

                @pl.when(me >= 1)
                def _():
                    w_copy(1, me + hop, s, me - 1).start()

    for peer in ch_c.peers():
        ch_c.arrived(ITERS - 1, peer, cbuf.at[ITERS - 1, peer])
    m_ref[...] = cbuf[ITERS - 1, :, 0].reshape(n, C)
    for hop in range(num_doc):
        for s in range(subs):

            @pl.when((me >= hop) & (me + 1 < num_doc))
            def _(hop=hop, s=s):
                w_copy(0, me - hop, s, me + 1).wait_send()

            @pl.when((me + hop < num_doc) & (me >= 1))
            def _(hop=hop, s=s):
                w_copy(1, me + hop, s, me - 1).wait_send()

    for channel in (ch_s, ch_y, ch_c, ch_p, ch_1, ch_2):
        channel.drain()


def per_device(documents, directions, phase, amplitude, doc_weight, labels):
    n, local_inputs = documents.shape
    input_rows, width_tile = directions.shape
    num_feat = lax.axis_size("feat")
    num_doc = lax.axis_size("doc")
    chunk = width_tile // num_doc
    subs = max(1, min(4, chunk // 128))
    share = n // num_feat
    f32, bf16 = jnp.float32, jnp.bfloat16
    vmem = pl.BlockSpec(memory_space=pltpu.VMEM)
    dma = pltpu.SemaphoreType.DMA
    shape = jax.ShapeDtypeStruct
    features, features_t, gram = pl.pallas_call(
        functools.partial(build_kernel, num_doc, num_feat, subs, (2.0 / width_tile) ** 0.5),
        out_shape=(
            shape((num_doc * n, chunk), f32),
            shape((chunk, num_doc * n), f32),
            shape((n, n), f32),
        ),
        in_specs=[vmem, pl.BlockSpec(memory_space=pl.ANY), vmem, vmem],
        out_specs=(vmem, vmem, vmem),
        scratch_shapes=[
            pltpu.VMEM((num_feat, n, local_inputs), bf16),
            pltpu.VMEM((num_doc, n, num_feat * local_inputs), bf16),
            pltpu.VMEM((num_doc, input_rows, chunk), bf16),
            pltpu.VMEM((num_doc, n, n), f32),
            pltpu.VMEM((num_doc, n, n), f32),
            dma((2, 1, num_feat)),
            dma((2, 1, num_doc)),
            dma((2, subs, num_doc)),
            dma((2, 1, num_doc)),
            dma,
        ],
        compiler_params=pltpu.CompilerParams(
            collective_id=0, has_side_effects=True, vmem_limit_bytes=48 * 1024 * 1024
        ),
        name="build",
    )(
        documents,
        directions,
        phase.reshape(num_doc, 1, chunk),
        amplitude.reshape(num_doc, 1, chunk),
    )
    eye = jnp.eye(n, dtype=f32)
    factor = jnp.linalg.cholesky(gram)
    lower_inv = lax.linalg.triangular_solve(factor, eye, left_side=True, lower=True)
    inverse = lax.dot_general(lower_inv, lower_inv, (((0,), (0,)), ((), ())), precision=HI)
    rounds = ITERS - 1
    return pl.pallas_call(
        functools.partial(admm_kernel, num_doc, num_feat, subs),
        out_shape=(shape((n, C), f32), shape((width_tile, C), f32)),
        in_specs=[vmem] * 5,
        out_specs=(vmem, vmem),
        scratch_shapes=[
            pltpu.VMEM((ITERS, num_doc, n, C), f32),
            pltpu.VMEM((ITERS, n, C), f32),
            pltpu.VMEM((ITERS, num_feat, share, C), f32),
            pltpu.VMEM((ITERS, num_feat, 2, share, C), f32),
            pltpu.VMEM((rounds, num_doc, n, C), f32),
            pltpu.VMEM((rounds, num_doc, n, C), f32),
            pltpu.VMEM((rounds, num_doc, 2, 8, C), f32),
            pltpu.VMEM((rounds, num_feat, 2, 8, C), f32),
            pltpu.VMEM((chunk, C), f32),
            pltpu.VMEM((chunk, C), f32),
            pltpu.VMEM((chunk, C), f32),
            dma((2, ITERS, num_doc)),
            dma((2, ITERS, num_feat)),
            dma((2, ITERS, num_feat)),
            dma((2, rounds, num_doc)),
            dma((2, rounds, num_doc)),
            dma((2, rounds, num_feat)),
            dma((2, 2, num_doc, subs)),
        ],
        compiler_params=pltpu.CompilerParams(
            collective_id=1, has_side_effects=True, vmem_limit_bytes=48 * 1024 * 1024
        ),
        name="admm",
    )(features, features_t, inverse, labels[:, None], doc_weight[:, None])


def solution(mesh):
    in_specs = (P("doc", "feat"), P("doc", "feat"), P("feat"), P("feat"), P("doc"), P("doc"))
    out_specs = (P("doc", None), P("feat", None))
    return jax.shard_map(
        per_device, mesh=mesh, in_specs=in_specs, out_specs=out_specs, check_vma=False
    )
```

```python
import functools

import jax
import jax.numpy as jnp
from jax import lax
from jax.experimental import pallas as pl
from jax.experimental.pallas import tpu as pltpu
from jax.sharding import PartitionSpec as P

C = 128
ITERS = 3
NEWTON = 3
HI = lax.Precision.HIGHEST
MESH = pl.DeviceIdType.MESH

shrink_level = 0.1
ratio_floor = 1e-06


def logistic_prox(target, signs, weight_ratio):
    current = target
    for newton_step in range(NEWTON):
        chance = 1.0 / (1.0 + jnp.exp(signs * current))
        gradient = current - target - weight_ratio * signs * chance
        current = current - gradient / (1.0 + weight_ratio * chance * (1.0 - chance))
    return current


def shrink_values(target, limit):
    return target - jnp.minimum(jnp.maximum(target, -limit), limit)


def cosine(angle):
    turns = jnp.floor(angle * 0.3183098861837907 + 0.5)
    rest = angle - turns * 3.140625
    rest = rest - turns * 9.67502593994140625e-4
    rest = rest - turns * 1.509957990978376432e-7
    odd = turns - 2.0 * jnp.floor(turns * 0.5)
    sq = rest * rest
    poly = 2.08767569878681e-9
    poly = poly * sq - 2.755731922398589e-7
    poly = poly * sq + 2.48015873015873e-5
    poly = poly * sq - 1.388888888888889e-3
    poly = poly * sq + 4.1666666666666664e-2
    poly = poly * sq - 0.5
    poly = poly * sq + 1.0
    return poly * (1.0 - 2.0 * odd)


def split(values):
    high = values.astype(jnp.bfloat16)
    return high, (values - high.astype(jnp.float32)).astype(jnp.bfloat16)


def split_dot(high, low, pair):
    both = jnp.dot(high, pair, preferred_element_type=jnp.float32)
    rest = jnp.dot(low, pair[:, :C], preferred_element_type=jnp.float32)
    return both[:, :C] + (both[:, C:] + rest)


def remote(src, dst, send_sem, recv_sem, axis, peer):
    return pltpu.make_async_remote_copy(
        src_ref=src,
        dst_ref=dst,
        send_sem=send_sem,
        recv_sem=recv_sem,
        device_id={axis: peer},
        device_id_type=MESH,
    )


def greet(num_doc, num_feat):
    barrier = pltpu.get_barrier_semaphore()
    for axis, size in (("doc", num_doc), ("feat", num_feat)):
        me = lax.axis_index(axis)
        for k in range(1, size):
            pl.semaphore_signal(
                barrier, inc=1, device_id={axis: lax.rem(me + k, size)}, device_id_type=MESH
            )
    pl.semaphore_wait(barrier, num_doc + num_feat - 2)


class Channel:
    def __init__(self, sems, axis, size):
        self.sems, self.axis, self.size = sems, axis, size
        self.me = lax.axis_index(axis)
        self.pending = []

    def peers(self):
        return [lax.rem(self.me + k, self.size) for k in range(1, self.size)]

    def send(self, slot, peer, src, dst):
        copy = remote(
            src, dst, self.sems.at[0, slot, peer], self.sems.at[1, slot, self.me], self.axis, peer
        )
        copy.start()
        self.pending.append(copy)

    def arrived(self, slot, peer, ref):
        remote(
            ref, ref, self.sems.at[0, slot, peer], self.sems.at[1, slot, peer], self.axis, peer
        ).wait_recv()

    def drain(self):
        for copy in self.pending:
            copy.wait_send()


def build_kernel(
    num_doc, num_feat, subs, scale,
    docs_ref, dir_ref, phase_hbm, amp_hbm,
    feat_ref, featt_ref, gram_ref,
    dpart, phase_ref, amp_ref, dirs, gsend, grecv,
    part_sems, row_sems, dir_sems, gram_sems, local_sem, table_sems,
):
    n = docs_ref.shape[0]
    chunk = dirs.shape[2]
    wide = chunk // subs
    me = lax.axis_index("doc")
    fme = lax.axis_index("feat")
    greet(num_doc, num_feat)
    ch_part = Channel(part_sems, "feat", num_feat)
    ch_row = Channel(row_sems, "doc", num_doc)
    ch_dir = Channel(dir_sems, "doc", num_doc)
    ch_gram = Channel(gram_sems, "doc", num_doc)
    for peer in ch_row.peers():
        ch_row.send(0, peer, docs_ref, dpart.at[fme, me])
    tables = [
        pltpu.make_async_copy(phase_hbm.at[me], phase_ref, table_sems.at[0]),
        pltpu.make_async_copy(amp_hbm.at[me], amp_ref, table_sems.at[1]),
    ]
    for table in tables:
        table.start()
    local = pltpu.make_async_copy(
        dir_ref.at[:, pl.ds(pl.multiple_of(me * chunk, chunk), chunk)], dirs.at[me], local_sem
    )
    local.start()
    for s in range(subs):
        for peer in ch_dir.peers():
            cols = pl.ds(pl.multiple_of(peer * chunk + s * wide, wide), wide)
            ch_dir.send(
                s, peer, dir_ref.at[:, cols], dirs.at[me, :, pl.ds(s * wide, wide)]
            )
    dpart[fme, me] = docs_ref[...]
    for peer in ch_row.peers():
        ch_row.arrived(0, peer, dpart.at[fme, peer])
    for peer in ch_part.peers():
        ch_part.send(0, peer, dpart.at[fme], dpart.at[fme])
    for peer in ch_part.peers():
        ch_part.arrived(0, peer, dpart.at[peer])
    full = jnp.concatenate(
        [
            dpart[k].reshape(num_doc * n, docs_ref.shape[1]).astype(jnp.float32)
            for k in range(num_feat)
        ],
        axis=1,
    ).astype(jnp.bfloat16)
    local.wait()
    for table in tables:
        table.wait()
    phase = phase_ref[...]
    amp = scale * amp_ref[...]
    for s in range(subs):
        cols = slice(s * wide, (s + 1) * wide)
        for peer in ch_dir.peers():
            ch_dir.arrived(s, peer, dirs.at[peer, :, pl.ds(s * wide, wide)])
        piece = dirs[:, :, cols].reshape(full.shape[1], wide)
        angles = jnp.dot(full, piece, preferred_element_type=jnp.float32)
        feats = amp[:, cols] * cosine(angles + phase[:, cols])
        flipped = feats.T
        feat_ref[0, :, cols], feat_ref[1, :, cols] = split(feats)
        featt_ref[0, cols, :], featt_ref[1, cols, :] = split(flipped)
        for i in range(num_doc):
            block = feats[i * n : (i + 1) * n]
            term = lax.dot_general(block, block, (((1,), (1,)), ((), ())), precision=HI)
            if s == 0:
                gsend[i] = term
            else:
                gsend[i] += term
    for peer in ch_gram.peers():
        ch_gram.send(0, peer, gsend.at[peer], grecv.at[me])
    grecv[me] = gsend[me]
    for peer in ch_gram.peers():
        ch_gram.arrived(0, peer, grecv.at[peer])
    total = grecv[0]
    for i in range(1, num_doc):
        total += grecv[i]
    rows = lax.broadcasted_iota(jnp.int32, (n, n), 0)
    cols = lax.broadcasted_iota(jnp.int32, (n, n), 1)
    gram_ref[...] = total + jnp.where(rows == cols, 1.0, 0.0)
    for channel in (ch_part, ch_row, ch_dir, ch_gram):
        channel.drain()


def sweep_kernel(gram_ref, inverse_ref):
    values = gram_ref[...]
    n = values.shape[0]
    lanes = lax.broadcasted_iota(jnp.int32, (1, n), 1)
    rows = lax.broadcasted_iota(jnp.int32, (n, 1), 0)
    for k in range(n):
        pivot = 1.0 / values[k : k + 1, k : k + 1]
        row = jnp.where(lanes == k, pivot, values[k : k + 1, :] * pivot)
        column = values[:, k : k + 1]
        values = jnp.where(
            rows == k, row, jnp.where(lanes == k, 0.0, values) - column * row
        )
    inverse_ref[...] = values


def fold(values):
    return jnp.sum(values.reshape(values.shape[0] // 8, 8, values.shape[1]), axis=0)


def total(values):
    return jnp.sum(jnp.sum(values, axis=0, keepdims=True), axis=1, keepdims=True)


def admm_kernel(
    num_doc, num_feat, subs,
    feat_ref, featt_ref, inv_ref, lab_ref, dw_ref,
    m_ref, w_ref,
    solved, part, yrecv, cbuf, psend, precv, sc1, sc2, z, lastmove, lastlift, signs_ref, weight_ref,
    s_sems, y_sems, c_sems, p_sems, sc1_sems, sc2_sems, w_sems,
):
    n = inv_ref.shape[0]
    chunk = z.shape[0]
    share = n // num_feat
    wide = chunk // subs
    me = lax.axis_index("doc")
    fme = lax.axis_index("feat")
    greet(num_doc, num_feat)
    ch_s = Channel(s_sems, "doc", num_doc)
    ch_y = Channel(y_sems, "feat", num_feat)
    ch_c = Channel(c_sems, "feat", num_feat)
    ch_p = Channel(p_sems, "doc", num_doc)
    ch_1 = Channel(sc1_sems, "doc", num_doc)
    ch_2 = Channel(sc2_sems, "feat", num_feat)
    classes = lax.broadcasted_iota(jnp.int32, (n, C), 1).astype(jnp.float32)
    spread = jnp.broadcast_to(lab_ref[...].astype(jnp.float32), (C, n)).T
    all_weight = jnp.broadcast_to(dw_ref[...], (C, n)).T
    all_signs = jnp.where(spread == classes, 1.0, -1.0)
    start = logistic_prox(jnp.zeros((n, C), jnp.float32), all_signs, all_weight)
    signs_ref[...] = all_signs
    weight_ref[...] = all_weight
    own = pl.ds(pl.multiple_of(fme * share, share), share)
    signs = signs_ref[own, :]
    weight = weight_ref[own, :]
    margins = logistic_prox(jnp.zeros((share, C), jnp.float32), signs, weight)
    duals = jnp.zeros((share, C), jnp.float32)
    rho = jnp.ones((1, 1), jnp.float32)
    inv = inv_ref[...]
    target = start / num_feat
    residue = target
    growth = None

    def my_rows(src, s):
        return pl.ds(pl.multiple_of(src * chunk + s * wide, wide), wide)

    def w_copy(direction, src, s, peer):
        ref = w_ref.at[my_rows(src, s), :]
        return remote(
            ref, ref, w_sems.at[direction, 0, src, s], w_sems.at[direction, 1, src, s], "doc", peer
        )

    for step in range(ITERS):
        last = step + 1 == ITERS
        answer = jnp.dot(inv, residue, precision=HI)
        applied = residue - answer
        new_part = target - answer
        solved[step, me] = answer
        part[step] = new_part
        for peer in ch_s.peers():
            ch_s.send(step, peer, solved.at[step, me], solved.at[step, me])
        for peer in ch_y.peers():
            rows = pl.ds(pl.multiple_of(peer * share, share), share)
            ch_y.send(step, peer, part.at[step, rows, :], yrecv.at[step, fme])
        yrecv[step, fme] = part[step, own, :]
        for peer in ch_y.peers():
            ch_y.arrived(step, peer, yrecv.at[step, peer])
        sums = yrecv[step, 0]
        for k in range(1, num_feat):
            sums += yrecv[step, k]
        old_margins = margins
        margins = logistic_prox(sums + duals, signs, weight / rho)
        duals = duals + sums - margins
        cbuf[step, fme, 0] = margins if last else (margins - sums) / num_feat
        cbuf[step, fme, 1] = duals / num_feat
        for peer in ch_c.peers():
            ch_c.send(step, peer, cbuf.at[step, fme], cbuf.at[step, fme])
        for peer in ch_s.peers():
            ch_s.arrived(step, peer, solved.at[step, peer])
        everything = jnp.concatenate(split(solved[step].reshape(num_doc * n, C)), axis=1)
        limit = shrink_level / (rho * num_doc)
        if not last:
            gap = fold((sums - margins) ** 2) if share > 8 else (sums - margins) ** 2
            shift = (
                fold((margins - old_margins) ** 2) if share > 8 else (margins - old_margins) ** 2
            )
            if step == 0:
                d_answer, d_applied = answer, applied
            else:
                d_answer = answer - last_answer / growth
                d_applied = applied - last_applied / growth
            primal = gap + fold(d_answer * d_applied)
            dual = shift
        for s in range(subs):
            rows = slice(s * wide, (s + 1) * wide)
            lift = split_dot(featt_ref[0, rows, :], featt_ref[1, rows, :], everything)
            if step == 0:
                fresh = shrink_values(lift / num_doc, limit)
                move = -fresh
                d_move, d_lift = move, lift
            else:
                old = z[rows, :]
                fresh = shrink_values(old + lift / num_doc, limit)
                if not last:
                    move = old - fresh
                    d_move = move - lastmove[rows, :] / growth
                    d_lift = lift - lastlift[rows, :] / growth
            if last:
                w_ref[my_rows(me, s), :] = num_feat * fresh

                @pl.when(me + 1 < num_doc)
                def _(s=s):
                    w_copy(0, me, s, me + 1).start()

                @pl.when(me >= 1)
                def _(s=s):
                    w_copy(1, me, s, me - 1).start()
            else:
                z[rows, :] = fresh
                lastmove[rows, :] = move
                lastlift[rows, :] = lift
                primal += fold(num_doc * d_move * d_move + 2.0 * d_move * d_lift)
                dual += num_doc * fold(move * move)
        if last:
            break
        sc1[step, me, 0] = primal
        sc1[step, me, 1] = dual
        for peer in ch_1.peers():
            ch_1.send(step, peer, sc1.at[step, me], sc1.at[step, me])
        weights = jnp.concatenate(split(z[...]), axis=1)
        for i in range(num_doc):
            block = slice(i * n, (i + 1) * n)
            psend[step, i] = split_dot(feat_ref[0, block, :], feat_ref[1, block, :], weights)
        for peer in ch_p.peers():
            ch_p.send(step, peer, psend.at[step, peer], precv.at[step, me])
        precv[step, me] = psend[step, me]
        for peer in ch_1.peers():
            ch_1.arrived(step, peer, sc1.at[step, peer])
        both = sc1[step, 0]
        for i in range(1, num_doc):
            both += sc1[step, i]
        sc2[step, fme] = both
        for peer in ch_2.peers():
            ch_2.send(step, peer, sc2.at[step, fme], sc2.at[step, fme])
        for peer in ch_2.peers():
            ch_2.arrived(step, peer, sc2.at[step, peer])
        both = sc2[step, 0]
        for k in range(1, num_feat):
            both += sc2[step, k]
        primal = jnp.maximum(total(both[0]), 0.0)
        dual = total(both[1])
        last_answer, last_applied = answer, applied
        for peer in ch_c.peers():
            ch_c.arrived(step, peer, cbuf.at[step, peer])
        growth = jnp.sqrt(
            jnp.sqrt((primal + ratio_floor) / (rho * rho * dual + ratio_floor))
        )
        rho = rho * growth
        duals = duals / growth
        fixed = cbuf[step, :, 0].reshape(n, C) - cbuf[step, :, 1].reshape(n, C) / growth
        target = new_part + fixed
        for peer in ch_p.peers():
            ch_p.arrived(step, peer, precv.at[step, peer])
        product = precv[step, 0]
        for i in range(1, num_doc):
            product += precv[step, i]
        previous = jnp.zeros((n, C), jnp.float32) if step == 0 else old_product
        residue = target - (product - (previous - product + applied) / growth)
        old_product = product
    for hop in range(1, num_doc):
        for s in range(subs):

            @pl.when(me >= hop)
            def _(hop=hop, s=s):
                w_copy(0, me - hop, s, me).wait_recv()

                @pl.when(me + 1 < num_doc)
                def _():
                    w_copy(0, me - hop, s, me + 1).start()

            @pl.when(me + hop < num_doc)
            def _(hop=hop, s=s):
                w_copy(1, me + hop, s, me).wait_recv()

                @pl.when(me >= 1)
                def _():
                    w_copy(1, me + hop, s, me - 1).start()

    for peer in ch_c.peers():
        ch_c.arrived(ITERS - 1, peer, cbuf.at[ITERS - 1, peer])
    m_ref[...] = cbuf[ITERS - 1, :, 0].reshape(n, C)
    for hop in range(num_doc):
        for s in range(subs):

            @pl.when((me >= hop) & (me + 1 < num_doc))
            def _(hop=hop, s=s):
                w_copy(0, me - hop, s, me + 1).wait_send()

            @pl.when((me + hop < num_doc) & (me >= 1))
            def _(hop=hop, s=s):
                w_copy(1, me + hop, s, me - 1).wait_send()

    for channel in (ch_s, ch_y, ch_c, ch_p, ch_1, ch_2):
        channel.drain()


def per_device(documents, directions, phase, amplitude, doc_weight, labels):
    n, local_inputs = documents.shape
    input_rows, width_tile = directions.shape
    num_feat = lax.axis_size("feat")
    num_doc = lax.axis_size("doc")
    chunk = width_tile // num_doc
    subs = max(1, min(4, chunk // 128))
    share = n // num_feat
    f32, bf16 = jnp.float32, jnp.bfloat16
    vmem = pl.BlockSpec(memory_space=pltpu.VMEM)
    dma = pltpu.SemaphoreType.DMA
    shape = jax.ShapeDtypeStruct
    features, features_t, gram = pl.pallas_call(
        functools.partial(build_kernel, num_doc, num_feat, subs, (2.0 / width_tile) ** 0.5),
        out_shape=(
            shape((2, num_doc * n, chunk), bf16),
            shape((2, chunk, num_doc * n), bf16),
            shape((n, n), f32),
        ),
        in_specs=[vmem] + [pl.BlockSpec(memory_space=pl.ANY)] * 3,
        out_specs=(vmem, vmem, vmem),
        scratch_shapes=[
            pltpu.VMEM((num_feat, num_doc, n, local_inputs), bf16),
            pltpu.VMEM((1, chunk), f32),
            pltpu.VMEM((1, chunk), f32),
            pltpu.VMEM((num_doc, input_rows, chunk), bf16),
            pltpu.VMEM((num_doc, n, n), f32),
            pltpu.VMEM((num_doc, n, n), f32),
            dma((2, 1, num_feat)),
            dma((2, 1, num_doc)),
            dma((2, subs, num_doc)),
            dma((2, 1, num_doc)),
            dma,
            dma((2,)),
        ],
        compiler_params=pltpu.CompilerParams(
            collective_id=0, has_side_effects=True, vmem_limit_bytes=48 * 1024 * 1024
        ),
        name="build",
    )(
        documents,
        directions,
        phase.reshape(num_doc, 1, chunk),
        amplitude.reshape(num_doc, 1, chunk),
    )
    inverse = pl.pallas_call(
        sweep_kernel,
        out_shape=shape((n, n), f32),
        in_specs=[vmem],
        out_specs=vmem,
        name="invert",
    )(gram)
    rounds = ITERS - 1
    return pl.pallas_call(
        functools.partial(admm_kernel, num_doc, num_feat, subs),
        out_shape=(shape((n, C), f32), shape((width_tile, C), f32)),
        in_specs=[vmem] * 5,
        out_specs=(vmem, vmem),
        scratch_shapes=[
            pltpu.VMEM((ITERS, num_doc, n, C), f32),
            pltpu.VMEM((ITERS, n, C), f32),
            pltpu.VMEM((ITERS, num_feat, share, C), f32),
            pltpu.VMEM((ITERS, num_feat, 2, share, C), f32),
            pltpu.VMEM((rounds, num_doc, n, C), f32),
            pltpu.VMEM((rounds, num_doc, n, C), f32),
            pltpu.VMEM((rounds, num_doc, 2, 8, C), f32),
            pltpu.VMEM((rounds, num_feat, 2, 8, C), f32),
            pltpu.VMEM((chunk, C), f32),
            pltpu.VMEM((chunk, C), f32),
            pltpu.VMEM((chunk, C), f32),
            pltpu.VMEM((n, C), f32),
            pltpu.VMEM((n, C), f32),
            dma((2, ITERS, num_doc)),
            dma((2, ITERS, num_feat)),
            dma((2, ITERS, num_feat)),
            dma((2, rounds, num_doc)),
            dma((2, rounds, num_doc)),
            dma((2, rounds, num_feat)),
            dma((2, 2, num_doc, subs)),
        ],
        compiler_params=pltpu.CompilerParams(
            collective_id=1, has_side_effects=True, vmem_limit_bytes=48 * 1024 * 1024
        ),
        name="admm",
    )(features, features_t, inverse, labels.reshape(1, n), doc_weight.reshape(1, n))


def solution(mesh):
    in_specs = (P("doc", "feat"), P("doc", "feat"), P("feat"), P("feat"), P("doc"), P("doc"))
    out_specs = (P("doc", None), P("feat", None))
    return jax.shard_map(
        per_device, mesh=mesh, in_specs=in_specs, out_specs=out_specs, check_vma=False
    )
```

```python
import functools

import jax
import jax.numpy as jnp
from jax import lax
from jax.experimental import pallas as pl
from jax.experimental.pallas import tpu as pltpu
from jax.sharding import PartitionSpec as P

C = 128
ITERS = 3
NEWTON = 3
HI = lax.Precision.HIGHEST
MESH = pl.DeviceIdType.MESH

shrink_level = 0.1
ratio_floor = 1e-06


def logistic_prox(target, signs, weight_ratio):
    current = target
    for newton_step in range(NEWTON):
        chance = 1.0 / (1.0 + jnp.exp(signs * current))
        gradient = current - target - weight_ratio * signs * chance
        current = current - gradient / (1.0 + weight_ratio * chance * (1.0 - chance))
    return current


def shrink_values(target, limit):
    return target - jnp.minimum(jnp.maximum(target, -limit), limit)


def cosine(angle):
    turns = jnp.floor(angle * 0.3183098861837907 + 0.5)
    rest = angle - turns * 3.140625
    rest = rest - turns * 9.67502593994140625e-4
    rest = rest - turns * 1.509957990978376432e-7
    odd = turns - 2.0 * jnp.floor(turns * 0.5)
    sq = rest * rest
    poly = 2.08767569878681e-9
    poly = poly * sq - 2.755731922398589e-7
    poly = poly * sq + 2.48015873015873e-5
    poly = poly * sq - 1.388888888888889e-3
    poly = poly * sq + 4.1666666666666664e-2
    poly = poly * sq - 0.5
    poly = poly * sq + 1.0
    return poly * (1.0 - 2.0 * odd)


def split(values):
    high = values.astype(jnp.bfloat16)
    return high, (values - high.astype(jnp.float32)).astype(jnp.bfloat16)


def split_dot(high, low, pair):
    both = jnp.dot(high, pair, preferred_element_type=jnp.float32)
    rest = jnp.dot(low, pair[:, :C], preferred_element_type=jnp.float32)
    return both[:, :C] + (both[:, C:] + rest)


def remote(src, dst, send_sem, recv_sem, axis, peer):
    return pltpu.make_async_remote_copy(
        src_ref=src,
        dst_ref=dst,
        send_sem=send_sem,
        recv_sem=recv_sem,
        device_id={axis: peer},
        device_id_type=MESH,
    )


def greet(num_doc, num_feat):
    barrier = pltpu.get_barrier_semaphore()
    for axis, size in (("doc", num_doc), ("feat", num_feat)):
        me = lax.axis_index(axis)
        for k in range(1, size):
            pl.semaphore_signal(
                barrier, inc=1, device_id={axis: lax.rem(me + k, size)}, device_id_type=MESH
            )
    pl.semaphore_wait(barrier, num_doc + num_feat - 2)


class Channel:
    def __init__(self, sems, axis, size):
        self.sems, self.axis, self.size = sems, axis, size
        self.me = lax.axis_index(axis)
        self.pending = []

    def peers(self):
        return [lax.rem(self.me + k, self.size) for k in range(1, self.size)]

    def send(self, slot, peer, src, dst):
        copy = remote(
            src, dst, self.sems.at[0, slot, peer], self.sems.at[1, slot, self.me], self.axis, peer
        )
        copy.start()
        self.pending.append(copy)

    def arrived(self, slot, peer, ref):
        remote(
            ref, ref, self.sems.at[0, slot, peer], self.sems.at[1, slot, peer], self.axis, peer
        ).wait_recv()

    def drain(self):
        for copy in self.pending:
            copy.wait_send()


def build_kernel(
    num_doc, num_feat, subs, scale,
    docs_ref, dir_ref, phase_hbm, amp_hbm,
    feat_ref, featt_ref, gram_ref,
    dpart, phase_ref, amp_ref, dirs, gsend, grecv,
    part_sems, row_sems, dir_sems, gram_sems, local_sem, table_sems,
):
    n = docs_ref.shape[0]
    chunk = dirs.shape[2]
    wide = chunk // subs
    me = lax.axis_index("doc")
    fme = lax.axis_index("feat")
    greet(num_doc, num_feat)
    ch_part = Channel(part_sems, "feat", num_feat)
    ch_row = Channel(row_sems, "doc", num_doc)
    ch_dir = Channel(dir_sems, "doc", num_doc)
    ch_gram = Channel(gram_sems, "doc", num_doc)
    for peer in ch_row.peers():
        ch_row.send(0, peer, docs_ref, dpart.at[fme, me])
    tables = [
        pltpu.make_async_copy(phase_hbm.at[me], phase_ref, table_sems.at[0]),
        pltpu.make_async_copy(amp_hbm.at[me], amp_ref, table_sems.at[1]),
    ]
    for table in tables:
        table.start()
    local = pltpu.make_async_copy(
        dir_ref.at[:, pl.ds(pl.multiple_of(me * chunk, chunk), chunk)], dirs.at[me], local_sem
    )
    local.start()
    for s in range(subs):
        for peer in ch_dir.peers():
            cols = pl.ds(pl.multiple_of(peer * chunk + s * wide, wide), wide)
            ch_dir.send(
                s, peer, dir_ref.at[:, cols], dirs.at[me, :, pl.ds(s * wide, wide)]
            )
    dpart[fme, me] = docs_ref[...]
    for peer in ch_row.peers():
        ch_row.arrived(0, peer, dpart.at[fme, peer])
    for peer in ch_part.peers():
        ch_part.send(0, peer, dpart.at[fme], dpart.at[fme])
    for peer in ch_part.peers():
        ch_part.arrived(0, peer, dpart.at[peer])
    full = jnp.concatenate(
        [
            dpart[k].reshape(num_doc * n, docs_ref.shape[1]).astype(jnp.float32)
            for k in range(num_feat)
        ],
        axis=1,
    ).astype(jnp.bfloat16)
    local.wait()
    for table in tables:
        table.wait()
    phase = phase_ref[...]
    amp = scale * amp_ref[...]
    for s in range(subs):
        cols = slice(s * wide, (s + 1) * wide)
        for peer in ch_dir.peers():
            ch_dir.arrived(s, peer, dirs.at[peer, :, pl.ds(s * wide, wide)])
        piece = dirs[:, :, cols].reshape(full.shape[1], wide)
        angles = jnp.dot(full, piece, preferred_element_type=jnp.float32)
        feats = amp[:, cols] * cosine(angles + phase[:, cols])
        flipped = feats.T
        feat_ref[0, :, cols], feat_ref[1, :, cols] = split(feats)
        featt_ref[0, cols, :], featt_ref[1, cols, :] = split(flipped)
        for i in range(num_doc):
            block = feats[i * n : (i + 1) * n]
            term = lax.dot_general(block, block, (((1,), (1,)), ((), ())), precision=HI)
            if s == 0:
                gsend[i] = term
            else:
                gsend[i] += term
    for peer in ch_gram.peers():
        ch_gram.send(0, peer, gsend.at[peer], grecv.at[me])
    grecv[me] = gsend[me]
    for peer in ch_gram.peers():
        ch_gram.arrived(0, peer, grecv.at[peer])
    total = grecv[0]
    for i in range(1, num_doc):
        total += grecv[i]
    rows = lax.broadcasted_iota(jnp.int32, (n, n), 0)
    cols = lax.broadcasted_iota(jnp.int32, (n, n), 1)
    gram_ref[...] = total + jnp.where(rows == cols, 1.0, 0.0)
    for channel in (ch_part, ch_row, ch_dir, ch_gram):
        channel.drain()


def sweep_kernel(gram_ref, inverse_ref):
    values = gram_ref[...]
    n = values.shape[0]
    lanes = lax.broadcasted_iota(jnp.int32, (1, n), 1)
    rows = lax.broadcasted_iota(jnp.int32, (n, 1), 0)
    for k in range(n):
        pivot = 1.0 / values[k : k + 1, k : k + 1]
        row = jnp.where(lanes == k, pivot, values[k : k + 1, :] * pivot)
        column = values[:, k : k + 1]
        values = jnp.where(
            rows == k, row, jnp.where(lanes == k, 0.0, values) - column * row
        )
    inverse_ref[...] = values


def fold(values):
    return jnp.sum(values.reshape(values.shape[0] // 8, 8, values.shape[1]), axis=0)


def total(values):
    return jnp.sum(jnp.sum(values, axis=0, keepdims=True), axis=1, keepdims=True)


def admm_kernel(
    num_doc, num_feat, subs,
    feat_ref, featt_ref, inv_ref, lab_ref, dw_ref,
    m_ref, w_ref,
    solved, part, yrecv, cbuf, psend, precv, sc1, sc2, z, lastmove, lastlift, signs_ref, weight_ref,
    s_sems, y_sems, c_sems, p_sems, sc1_sems, sc2_sems, w_sems,
):
    n = inv_ref.shape[0]
    chunk = z.shape[0]
    share = n // num_feat
    wide = chunk // subs
    me = lax.axis_index("doc")
    fme = lax.axis_index("feat")
    ch_s = Channel(s_sems, "doc", num_doc)
    ch_y = Channel(y_sems, "feat", num_feat)
    ch_c = Channel(c_sems, "feat", num_feat)
    ch_p = Channel(p_sems, "doc", num_doc)
    ch_1 = Channel(sc1_sems, "doc", num_doc)
    ch_2 = Channel(sc2_sems, "feat", num_feat)
    classes = lax.broadcasted_iota(jnp.int32, (n, C), 1).astype(jnp.float32)
    spread = jnp.broadcast_to(lab_ref[...].astype(jnp.float32), (C, n)).T
    all_weight = jnp.broadcast_to(dw_ref[...], (C, n)).T
    all_signs = jnp.where(spread == classes, 1.0, -1.0)
    start = logistic_prox(jnp.zeros((n, C), jnp.float32), all_signs, all_weight)
    signs_ref[...] = all_signs
    weight_ref[...] = all_weight
    own = pl.ds(pl.multiple_of(fme * share, share), share)
    signs = signs_ref[own, :]
    weight = weight_ref[own, :]
    margins = logistic_prox(jnp.zeros((share, C), jnp.float32), signs, weight)
    duals = jnp.zeros((share, C), jnp.float32)
    rho = jnp.ones((1, 1), jnp.float32)
    inv = inv_ref[...]
    target = start / num_feat
    residue = target
    growth = None

    def my_rows(src, s):
        return pl.ds(pl.multiple_of(src * chunk + s * wide, wide), wide)

    def w_copy(direction, src, s, peer):
        ref = w_ref.at[my_rows(src, s), :]
        return remote(
            ref, ref, w_sems.at[direction, 0, src, s], w_sems.at[direction, 1, src, s], "doc", peer
        )

    for step in range(ITERS):
        last = step + 1 == ITERS
        answer = jnp.dot(inv, residue, precision=HI)
        applied = residue - answer
        new_part = target - answer
        solved[step, me] = answer
        part[step] = new_part
        for peer in ch_s.peers():
            ch_s.send(step, peer, solved.at[step, me], solved.at[step, me])
        for peer in ch_y.peers():
            rows = pl.ds(pl.multiple_of(peer * share, share), share)
            ch_y.send(step, peer, part.at[step, rows, :], yrecv.at[step, fme])
        yrecv[step, fme] = part[step, own, :]
        for peer in ch_y.peers():
            ch_y.arrived(step, peer, yrecv.at[step, peer])
        sums = yrecv[step, 0]
        for k in range(1, num_feat):
            sums += yrecv[step, k]
        old_margins = margins
        margins = logistic_prox(sums + duals, signs, weight / rho)
        duals = duals + sums - margins
        cbuf[step, fme, 0] = margins if last else (margins - sums) / num_feat
        cbuf[step, fme, 1] = duals / num_feat
        for peer in ch_c.peers():
            ch_c.send(step, peer, cbuf.at[step, fme], cbuf.at[step, fme])
        for peer in ch_s.peers():
            ch_s.arrived(step, peer, solved.at[step, peer])
        everything = jnp.concatenate(split(solved[step].reshape(num_doc * n, C)), axis=1)
        limit = shrink_level / (rho * num_doc)
        if not last:
            gap = fold((sums - margins) ** 2) if share > 8 else (sums - margins) ** 2
            shift = (
                fold((margins - old_margins) ** 2) if share > 8 else (margins - old_margins) ** 2
            )
            if step == 0:
                d_answer, d_applied = answer, applied
            else:
                d_answer = answer - last_answer / growth
                d_applied = applied - last_applied / growth
            primal = gap + fold(d_answer * d_applied)
            dual = shift
        for s in range(subs):
            rows = slice(s * wide, (s + 1) * wide)
            lift = split_dot(featt_ref[0, rows, :], featt_ref[1, rows, :], everything)
            if step == 0:
                fresh = shrink_values(lift / num_doc, limit)
                move = -fresh
                d_move, d_lift = move, lift
            else:
                old = z[rows, :]
                fresh = shrink_values(old + lift / num_doc, limit)
                if not last:
                    move = old - fresh
                    d_move = move - lastmove[rows, :] / growth
                    d_lift = lift - lastlift[rows, :] / growth
            if last:
                w_ref[my_rows(me, s), :] = num_feat * fresh

                @pl.when(me + 1 < num_doc)
                def _(s=s):
                    w_copy(0, me, s, me + 1).start()

                @pl.when(me >= 1)
                def _(s=s):
                    w_copy(1, me, s, me - 1).start()
            else:
                z[rows, :] = fresh
                lastmove[rows, :] = move
                lastlift[rows, :] = lift
                primal += fold(num_doc * d_move * d_move + 2.0 * d_move * d_lift)
                dual += num_doc * fold(move * move)
        if last:
            break
        sc1[step, me, 0] = primal
        sc1[step, me, 1] = dual
        for peer in ch_1.peers():
            ch_1.send(step, peer, sc1.at[step, me], sc1.at[step, me])
        weights = jnp.concatenate(split(z[...]), axis=1)
        for i in range(num_doc):
            block = slice(i * n, (i + 1) * n)
            psend[step, i] = split_dot(feat_ref[0, block, :], feat_ref[1, block, :], weights)
        for peer in ch_p.peers():
            ch_p.send(step, peer, psend.at[step, peer], precv.at[step, me])
        precv[step, me] = psend[step, me]
        for peer in ch_1.peers():
            ch_1.arrived(step, peer, sc1.at[step, peer])
        both = sc1[step, 0]
        for i in range(1, num_doc):
            both += sc1[step, i]
        sc2[step, fme] = both
        for peer in ch_2.peers():
            ch_2.send(step, peer, sc2.at[step, fme], sc2.at[step, fme])
        for peer in ch_2.peers():
            ch_2.arrived(step, peer, sc2.at[step, peer])
        both = sc2[step, 0]
        for k in range(1, num_feat):
            both += sc2[step, k]
        primal = jnp.maximum(total(both[0]), 0.0)
        dual = total(both[1])
        last_answer, last_applied = answer, applied
        for peer in ch_c.peers():
            ch_c.arrived(step, peer, cbuf.at[step, peer])
        growth = jnp.sqrt(
            jnp.sqrt((primal + ratio_floor) / (rho * rho * dual + ratio_floor))
        )
        rho = rho * growth
        duals = duals / growth
        fixed = cbuf[step, :, 0].reshape(n, C) - cbuf[step, :, 1].reshape(n, C) / growth
        target = new_part + fixed
        for peer in ch_p.peers():
            ch_p.arrived(step, peer, precv.at[step, peer])
        product = precv[step, 0]
        for i in range(1, num_doc):
            product += precv[step, i]
        previous = jnp.zeros((n, C), jnp.float32) if step == 0 else old_product
        residue = target - (product - (previous - product + applied) / growth)
        old_product = product
    for hop in range(1, num_doc):
        for s in range(subs):

            @pl.when(me >= hop)
            def _(hop=hop, s=s):
                w_copy(0, me - hop, s, me).wait_recv()

                @pl.when(me + 1 < num_doc)
                def _():
                    w_copy(0, me - hop, s, me + 1).start()

            @pl.when(me + hop < num_doc)
            def _(hop=hop, s=s):
                w_copy(1, me + hop, s, me).wait_recv()

                @pl.when(me >= 1)
                def _():
                    w_copy(1, me + hop, s, me - 1).start()

    for peer in ch_c.peers():
        ch_c.arrived(ITERS - 1, peer, cbuf.at[ITERS - 1, peer])
    m_ref[...] = cbuf[ITERS - 1, :, 0].reshape(n, C)
    for hop in range(num_doc):
        for s in range(subs):

            @pl.when((me >= hop) & (me + 1 < num_doc))
            def _(hop=hop, s=s):
                w_copy(0, me - hop, s, me + 1).wait_send()

            @pl.when((me + hop < num_doc) & (me >= 1))
            def _(hop=hop, s=s):
                w_copy(1, me + hop, s, me - 1).wait_send()

    for channel in (ch_s, ch_y, ch_c, ch_p, ch_1, ch_2):
        channel.drain()


def whole_kernel(
    num_doc, num_feat, subs, scale,
    docs_ref, dir_ref, phase_hbm, amp_hbm, lab_ref, dw_ref,
    m_ref, w_ref,
    feat_ref, featt_ref, gram_ref, inv_ref,
    *scratch,
):
    build_kernel(
        num_doc, num_feat, subs, scale,
        docs_ref, dir_ref, phase_hbm, amp_hbm, feat_ref, featt_ref, gram_ref, *scratch[:12],
    )
    sweep_kernel(gram_ref, inv_ref)
    admm_kernel(
        num_doc, num_feat, subs,
        feat_ref, featt_ref, inv_ref, lab_ref, dw_ref, m_ref, w_ref, *scratch[12:],
    )


def per_device(documents, directions, phase, amplitude, doc_weight, labels):
    n, local_inputs = documents.shape
    input_rows, width_tile = directions.shape
    num_feat = lax.axis_size("feat")
    num_doc = lax.axis_size("doc")
    chunk = width_tile // num_doc
    subs = max(1, min(4, chunk // 128))
    share = n // num_feat
    f32, bf16 = jnp.float32, jnp.bfloat16
    vmem = pl.BlockSpec(memory_space=pltpu.VMEM)
    dma = pltpu.SemaphoreType.DMA
    shape = jax.ShapeDtypeStruct
    rounds = ITERS - 1
    any_space = pl.BlockSpec(memory_space=pl.ANY)
    return pl.pallas_call(
        functools.partial(
            whole_kernel, num_doc, num_feat, subs, (2.0 / width_tile) ** 0.5
        ),
        out_shape=(shape((n, C), f32), shape((width_tile, C), f32)),
        in_specs=[vmem, any_space, any_space, any_space, vmem, vmem],
        out_specs=(vmem, vmem),
        scratch_shapes=[
            pltpu.VMEM((2, num_doc * n, chunk), bf16),
            pltpu.VMEM((2, chunk, num_doc * n), bf16),
            pltpu.VMEM((n, n), f32),
            pltpu.VMEM((n, n), f32),
            pltpu.VMEM((num_feat, num_doc, n, local_inputs), bf16),
            pltpu.VMEM((1, chunk), f32),
            pltpu.VMEM((1, chunk), f32),
            pltpu.VMEM((num_doc, input_rows, chunk), bf16),
            pltpu.VMEM((num_doc, n, n), f32),
            pltpu.VMEM((num_doc, n, n), f32),
            dma((2, 1, num_feat)),
            dma((2, 1, num_doc)),
            dma((2, subs, num_doc)),
            dma((2, 1, num_doc)),
            dma,
            dma((2,)),
            pltpu.VMEM((ITERS, num_doc, n, C), f32),
            pltpu.VMEM((ITERS, n, C), f32),
            pltpu.VMEM((ITERS, num_feat, share, C), f32),
            pltpu.VMEM((ITERS, num_feat, 2, share, C), f32),
            pltpu.VMEM((rounds, num_doc, n, C), f32),
            pltpu.VMEM((rounds, num_doc, n, C), f32),
            pltpu.VMEM((rounds, num_doc, 2, 8, C), f32),
            pltpu.VMEM((rounds, num_feat, 2, 8, C), f32),
            pltpu.VMEM((chunk, C), f32),
            pltpu.VMEM((chunk, C), f32),
            pltpu.VMEM((chunk, C), f32),
            pltpu.VMEM((n, C), f32),
            pltpu.VMEM((n, C), f32),
            dma((2, ITERS, num_doc)),
            dma((2, ITERS, num_feat)),
            dma((2, ITERS, num_feat)),
            dma((2, rounds, num_doc)),
            dma((2, rounds, num_doc)),
            dma((2, rounds, num_feat)),
            dma((2, 2, num_doc, subs)),
        ],
        compiler_params=pltpu.CompilerParams(
            collective_id=0, has_side_effects=True, vmem_limit_bytes=48 * 1024 * 1024
        ),
        name="admm",
    )(
        documents,
        directions,
        phase.reshape(num_doc, 1, chunk),
        amplitude.reshape(num_doc, 1, chunk),
        labels.reshape(1, n),
        doc_weight.reshape(1, n),
    )


def solution(mesh):
    in_specs = (P("doc", "feat"), P("doc", "feat"), P("feat"), P("feat"), P("doc"), P("doc"))
    out_specs = (P("doc", None), P("feat", None))
    return jax.shard_map(
        per_device, mesh=mesh, in_specs=in_specs, out_specs=out_specs, check_vma=False
    )
```
